32 devices in a mesh: width: 4 (over y, core), hidden: 8 (over z, x).
Axes of the slice: x: 2, y: 2, z: 4, core: 2. Of those that a mesh axis runs over, the one named last changes fastest.
Arguments:
- tokens: bfloat16 [1152, 5120], P(None, 'width'), may hold values from -6 to 6
- cotangent: bfloat16 [1152, 5120], P(None, 'width'), may hold values from -6 to 6
- w_up: bfloat16 [5120, 13824], P('width', 'hidden'), may hold values from -0.078125 to 0.078125
- bias_up: float32 [13824], P('hidden'), may hold values from -3 to 3
- w_down: bfloat16 [13824, 5120], P('hidden', 'width'), may hold values from -0.0546875 to 0.0546875
- mod_table: float32 [32, 3, 5120], P(None, None, 'width'), may hold values from -3 to 3
- seg_ids: int32 [1152], replicated, may hold values from 0 to 15, never falling along the last dimension, each value on 1 to 144 neighbouring positions
- step_ids: int32 [16], replicated, may hold values from 0 to 31
Outputs:
- grad_x: bfloat16 [1152, 5120], P(None, 'width')
- grad_up: float32 [5120, 13824], P('width', 'hidden')
- grad_down: float32 [13824, 5120], P('hidden', 'width')
- grad_bias: float32 [13824], P('hidden')
- grad_table: float32 [32, 3, 5120], P(None, None, 'width')
The draws below stay inside these ranges and needn't reach their ends.
Inputs may be any that keep to these rules, and one draw needn't show every extreme that they name: `seg_ids`: request numbers never fall along the tokens and every request holds at least one token.
All inputs are finite; a program needn't handle non-finite values.
Results may differ from the reference program's by a relative error of at most 0.0063.
Values may be sent and summed in bfloat16 or wider, within the bound.
No kernel may reach another device: no remote copies, remote signals or barrier semaphores. Data moves between devices by JAX's collectives and lax.ppermute only.
A program may use at most 128 MiB of HBM per device.

```python
import math
import jax
import jax.numpy as jnp
import numpy as np
from jax import lax

D = 5120
FF = 13824
TOKENS = 1152
REQUESTS = 16
NSTEPS = 32


def plant(array, rng, smallest, high):
    spot = [jax.random.randint(jax.random.fold_in(rng, axis), (), 0, length) for axis, length in enumerate(array.shape)]
    widest = array.shape.index(max(array.shape))
    next_to = spot[:widest] + [(spot[widest] + 1) % array.shape[widest]] + spot[widest + 1:]
    return array.at[tuple(spot)].set(smallest).at[tuple(next_to)].set(high)


def block_scale(rng, shape, split, smallest, top_value):
    def one(position, parts):
        heights = jax.random.uniform(jax.random.fold_in(jax.random.fold_in(rng, 6), position), (parts,), jnp.float32, smallest / len(split), top_value / len(split))
        return jnp.repeat(jnp.exp(heights), shape[position] // parts).reshape((-1,) + (1,) * (len(shape) - position - 1))

    factor_of = one(*split[0])
    for cut in split[1:]:
        factor_of = factor_of * one(*cut)
    return factor_of


def length_profile(amount, total, limit, lean):
    loads = [(1 << 20) // math.isqrt(grade ** lean) + 1 for grade in range(2, amount + 1)]
    rest, counts = total - limit - (amount - 1), [1] * (amount - 1)
    while rest > 0:
        movable = [i for i in range(amount - 1) if counts[i] < limit]
        whole, left = sum([loads[i] for i in movable]), rest
        for i in movable:
            addition = min(limit - counts[i], max(1, left * loads[i] // whole), rest)
            counts[i] = counts[i] + addition
            rest = rest - addition
    return np.array([limit] + counts)


def ragged_sizes(stream_key, count, total, limit, skew):
    if count == 2:
        one = jax.random.randint(stream_key, (), max(1, total - limit), min(limit, total - 1) + 1)
        return jnp.stack([one, total - one])
    lengths = jnp.asarray(length_profile(count, total, limit, skew), jnp.int32)
    pairs = (count - 1) // 2
    giver, taker = lengths[1:1 + 2 * pairs:2], lengths[2:2 + 2 * pairs:2]
    slack = jnp.minimum(giver - 1, limit - taker)
    shifted = jax.random.randint(jax.random.fold_in(stream_key, 1), (pairs,), 0, 1 << 20) % (slack + 1)
    lengths = lengths.at[1:1 + 2 * pairs:2].set(giver - shifted).at[2:2 + 2 * pairs:2].set(taker + shifted)
    return lengths[jax.random.permutation(jax.random.fold_in(stream_key, 2), count)]


def bell_draw(rng, extent, width, limit, cuts=(), dtype=jnp.bfloat16):
    entries = width * jax.random.normal(rng, extent, jnp.float32)
    if cuts:
        entries = entries * block_scale(rng, extent, cuts, -0.22, 0.18)
    return jnp.clip(entries, -limit, limit).astype(dtype)


def setup_inputs(seed: int = 0) -> dict:
    key_list = jax.random.split(jax.random.key(seed), 9)
    tokens = bell_draw(key_list[0], (TOKENS, D), 1.0, 6.0, ((1, 4),))
    cotangent = bell_draw(key_list[1], (TOKENS, D), 1.0, 6.0, ((1, 4),))
    w_up = bell_draw(key_list[2], (D, FF), D ** -0.5, 0.078125, ((0, 4), (1, 8)))
    bias_up = bell_draw(key_list[3], (FF,), 0.5, 3.0, ((0, 8),), jnp.float32)
    w_down = bell_draw(key_list[4], (FF, D), FF ** -0.5, 0.0546875, ((0, 8), (1, 4)))
    mod_table = bell_draw(key_list[5], (NSTEPS, 3, D), 0.5, 3.0, ((2, 4),), jnp.float32)
    seg_ids = jnp.searchsorted(jnp.cumsum(ragged_sizes(key_list[6], REQUESTS, TOKENS, TOKENS // 8, 1)), jnp.arange(TOKENS), side="right").astype(jnp.int32)
    step_ids = plant(jax.random.randint(key_list[7], (REQUESTS,), 0, NSTEPS), jax.random.fold_in(key_list[7], 1), 0, NSTEPS - 1).astype(jnp.int32)
    return {"tokens": tokens, "cotangent": cotangent, "w_up": w_up, "bias_up": bias_up, "w_down": w_down, "mod_table": mod_table, "seg_ids": seg_ids, "step_ids": step_ids}


def gelu_tanh(value):
    return jax.nn.gelu(value, approximate=True)

def reference(tokens, cotangent, w_up, bias_up, w_down, mod_table, seg_ids, step_ids):
    highest = lax.Precision.HIGHEST
    req_of = (seg_ids[:, None] == jnp.arange(REQUESTS)[None, :]).astype(jnp.float32)
    step_of = (step_ids[:, None] == jnp.arange(NSTEPS)[None, :]).astype(jnp.float32)
    req_mod = jnp.einsum('rk,kcd->rcd', step_of, mod_table, precision=highest)
    shift_tok = jnp.dot(req_of, req_mod[:, 0], precision=highest)
    scale_tok = jnp.dot(req_of, req_mod[:, 1], precision=highest)
    gate_tok = jnp.dot(req_of, req_mod[:, 2], precision=highest)
    x_full = tokens.astype(jnp.float32)
    tok_mean = lax.optimization_barrier(jnp.sum(x_full, 1)) / D
    tok_var = lax.optimization_barrier(jnp.sum(x_full * x_full, 1)) / D - tok_mean * tok_mean
    inv_std = lax.rsqrt(tok_var + 1e-06)
    x_hat = (x_full - tok_mean[:, None]) * inv_std[:, None]
    mod_gain = 1.0 + scale_tok
    normed = (x_hat * mod_gain + shift_tok).astype(jnp.bfloat16)
    pre_act = jnp.dot(normed, w_up, preferred_element_type=jnp.float32) + bias_up
    hidden_act = gelu_tanh(pre_act).astype(jnp.bfloat16)
    y_out = jnp.dot(hidden_act, w_down, preferred_element_type=jnp.float32)
    grad_gate_req = jnp.dot(req_of.T, cotangent.astype(jnp.float32) * y_out, precision=highest)
    d_out = (cotangent.astype(jnp.float32) * gate_tok).astype(jnp.bfloat16)
    d_act = jnp.dot(d_out, w_down.T, preferred_element_type=jnp.float32)
    _, pull = jax.vjp(gelu_tanh, pre_act)
    d_pre = pull(d_act)[0]
    d_pre_b = d_pre.astype(jnp.bfloat16)
    grad_bias = lax.optimization_barrier(jnp.sum(d_pre, 0))
    grad_down = jnp.dot(hidden_act.T, d_out, preferred_element_type=jnp.float32)
    grad_up = jnp.dot(normed.T, d_pre_b, preferred_element_type=jnp.float32)
    d_norm = jnp.dot(d_pre_b, w_up.T, preferred_element_type=jnp.float32)
    grad_shift_req = jnp.dot(req_of.T, d_norm, precision=highest)
    grad_scale_req = jnp.dot(req_of.T, d_norm * x_hat, precision=highest)
    req_grads = jnp.stack([grad_shift_req, grad_scale_req, grad_gate_req], 1)
    grad_table = jnp.einsum('rk,rcd->kcd', step_of, req_grads, precision=highest)
    d_hat = d_norm * mod_gain
    mean_one = lax.optimization_barrier(jnp.sum(d_hat, 1)) / D
    mean_two = lax.optimization_barrier(jnp.sum(d_hat * x_hat, 1)) / D
    grad_x = cotangent.astype(jnp.float32) + inv_std[:, None] * (d_hat - mean_one[:, None] - x_hat * mean_two[:, None])
    return (grad_x.astype(jnp.bfloat16), grad_up, grad_down, grad_bias, grad_table)
```

```python
import functools

import jax
import jax.numpy as jnp
from jax import lax
from jax.experimental import pallas as pl
from jax.experimental.pallas import tpu as pltpu
from jax.sharding import PartitionSpec as P


SPLIT = (3, 3, 2, 1)
TILE = 64
BLOCK_N = 256
BLOCK_D = 256
PLAN = tuple(
    (word.rstrip("0123456789"), int(word[-1]))
    for line in (
        "mid0 part0 mid1 ra0",
        "part1 rb0 mid2 mid3",
        "part2 ra1 na0 part3",
        "nb0 rb1 ra2 ra3",
        "gate0 ga0 rb2 rb3",
        "na1 down0 gb0 na2",
        "nb1 na3 nb2 nb3",
        "ga1 up0 ga2 ga3",
        "gb1 gb2 gb3",
        "fin0 fin1 fin2 fin3",
    )
    for word in line.split()
)


def f32(value):
    return value.astype(jnp.float32)


def bf16(value):
    return value.astype(jnp.bfloat16)


def swap(value, axis, mask, size):
    return lax.ppermute(value, axis, [(i, i ^ mask) for i in range(size)])


def sum_all(value, axis, size):
    terms = [value] + [swap(value, axis, mask, size) for mask in range(1, size)]
    while len(terms) > 1:
        terms = [terms[i] + terms[i + 1] for i in range(0, len(terms), 2)]
    return terms[0]


def sum_pairs(value, axis, mask, size):
    while mask < size:
        value = value + swap(value, axis, mask, size)
        mask *= 2
    return value


def round_off(value):
    return lax.reduce_precision(value, 8, 7)


def three_parts(value):
    first = round_off(value)
    second = round_off(value - first)
    third = value - first - second
    return bf16(jnp.concatenate([first, second, third], 0))


def mm(a, b, dims):
    return lax.dot_general(a, b, (dims, ((), ())), preferred_element_type=jnp.float32)


def tie(values, other):
    values = list(values)
    *values, _ = lax.optimization_barrier((*values, other))
    return values


def look(seg, table):
    wide = table.shape[0]
    reqs = wide // 3
    lanes = lax.broadcasted_iota(jnp.int32, (seg.shape[0], wide), 1)
    hot = (lanes == seg) | (lanes == seg + reqs) | (lanes == seg + 2 * reqs)
    return mm(jnp.where(hot, 1.0, 0.0).astype(jnp.bfloat16), table, ((1,), (0,)))


def call(kernel, grid, prefetch, in_specs, out_specs, out_shape, cost, aliases=None):
    return pl.pallas_call(
        kernel,
        out_shape=out_shape,
        grid_spec=pltpu.PrefetchScalarGridSpec(
            num_scalar_prefetch=prefetch, grid=grid, in_specs=in_specs, out_specs=out_specs
        ),
        input_output_aliases=aliases or {},
        cost_estimate=pl.CostEstimate(flops=cost[0], bytes_accessed=cost[1], transcendentals=0),
    )


def shape(dims, dtype=jnp.bfloat16):
    return jax.ShapeDtypeStruct(dims, dtype)


def project_pieces(pieces, lhs, w, outs):
    total = bf16(mm(lhs[...], w[...], ((1,), (1,))))
    for (start, size), out in zip(pieces, outs):
        out[...] = total[start:start + size]


def project_d_kernel(pieces, order, dep, cot, seg, gate, w, lhs, cot_out, hot_out, *outs):
    @pl.when(pl.program_id(0) == 0)
    def _():
        def step(t, carry):
            src = pl.ds(pl.multiple_of(order[t] * TILE, TILE), TILE)
            dst = pl.ds(pl.multiple_of(t * TILE, TILE), TILE)
            ids = seg[src, :]
            value = cot[src, :]
            lhs[dst, :] = bf16(f32(value) * look(ids, gate[...]))
            cot_out[dst, :] = value
            lanes = lax.broadcasted_iota(jnp.int32, (TILE, hot_out.shape[1]), 1)
            hot_out[dst, :] = jnp.where(lanes == ids, 1.0, 0.0).astype(jnp.bfloat16)
            return carry

        lax.fori_loop(0, lhs.shape[0] // TILE, step, 0)

    project_pieces(pieces, lhs, w, outs)


def project_u_kernel(pieces, order, dep, tok, seg, st, shift, scale, w, lhs, *outs):
    @pl.when(pl.program_id(0) == 0)
    def _():
        def step(t, carry):
            src = pl.ds(pl.multiple_of(order[t] * TILE, TILE), TILE)
            dst = pl.ds(pl.multiple_of(t * TILE, TILE), TILE)
            ids = seg[src, :]
            x_hat = (f32(tok[src, :]) - st[src, 0:1]) * st[src, 1:2]
            lhs[dst, :] = bf16(x_hat * (1.0 + look(ids, scale[...])) + look(ids, shift[...]))
            return carry

        lax.fori_loop(0, lhs.shape[0] // TILE, step, 0)

    project_pieces(pieces, lhs, w, outs)


def mid_kernel(dep, ds, dr, us, ur, bias, out, total):
    value = f32(us[...]) + f32(ur[...]) + bias[...]
    root = 0.7978845608028654
    square = value * value
    bent = jnp.tanh(root * (value + 0.044715 * (value * square)))
    half = 0.5 * (1.0 + bent)
    slope = half + 0.5 * value * (1.0 - bent * bent) * (root * (1.0 + 0.134145 * square))
    d_pre = (f32(ds[...]) + f32(dr[...])) * slope
    out[0] = bf16(value * half)
    out[1] = bf16(d_pre)

    @pl.when(pl.program_id(0) == 0)
    def _():
        total[...] = jnp.zeros_like(total)

    total[...] += jnp.sum(d_pre, 0, keepdims=True)


def part_kernel(first, flags, dep, own, oth, w, *refs):
    send, keep, act_all, grad_all = refs[0 if first else 2:]
    half = own.shape[1]

    @pl.when(pl.program_id(0) == 0)
    def _():
        for side, ref in enumerate((own, oth)):
            act_all[side * half:(side + 1) * half, :] = ref[0]
            grad_all[side * half:(side + 1) * half, :] = ref[1]

    total = bf16(mm(grad_all[...], w[...], ((1,), (0,))))

    @pl.when(flags[0] == 1)
    def _():
        send[...] = total[half:]
        keep[...] = total[:half]

    @pl.when(flags[0] == 0)
    def _():
        send[...] = total[:half]
        keep[...] = total[half:]


def norm_a_kernel(q, dep, keep, got, tok, st, seg, scale, sums, table):
    d = keep[...] + f32(got[...])
    x_hat = (f32(tok[...]) - st[:, 0:1]) * st[:, 1:2]
    d_hat = d * (1.0 + look(seg[...], scale[...]))
    one = jnp.sum(d_hat, 1, keepdims=True)
    two = jnp.sum(d_hat * x_hat, 1, keepdims=True)
    lane = lax.broadcasted_iota(jnp.int32, sums.shape, 1)
    sums[...] = jnp.where(lane == 0, one, jnp.where(lane == 1, two, 0.0))
    reqs = table.shape[1]
    ids = lax.broadcasted_iota(jnp.int32, (d.shape[0], reqs), 1)
    hot = jnp.where(ids == seg[...], 1.0, 0.0).astype(jnp.bfloat16)
    for c, value in enumerate((d, d * x_hat)):
        top = bf16(value)
        low = bf16(value - f32(top))
        table[c] = mm(hot, top, ((0,), (0,))) + mm(hot, low, ((0,), (0,)))


def norm_b_kernel(dim, q, dep, keep, got, tok, cot, st, seg, scale, sums, out):
    d = keep[...] + f32(got[...])
    inv = st[:, 1:2]
    x_hat = (f32(tok[...]) - st[:, 0:1]) * inv
    d_hat = d * (1.0 + look(seg[...], scale[...]))
    means = sums[...] * (1.0 / dim)
    out[...] = bf16(f32(cot[...]) + inv * (d_hat - means[:, 0:1] - x_hat * means[:, 1:2]))


def make_body(nw, nh):
    def body(tokens, cotangent, w_up, bias_up, w_down, mod_table, seg_ids, step_ids):
        count, dw = tokens.shape
        fh = w_up.shape[1]
        dim = dw * nw
        reqs, rows_of = step_ids.shape[0], mod_table.shape[0]
        highest = lax.Precision.HIGHEST
        core = lax.axis_index("width") % 2
        me = lax.axis_index("hidden")
        step_of = f32(step_ids[:, None] == jnp.arange(rows_of)[None, :])
        req_mod = jnp.einsum("rk,kcd->crd", step_of, mod_table, precision=highest)
        shift3, scale3, gate3 = [three_parts(req_mod[c]) for c in range(3)]
        seg = seg_ids[:, None]

        x_full = f32(tokens)
        moments = jnp.stack([jnp.sum(x_full, 1), jnp.sum(x_full * x_full, 1)])
        sums = sum_all(moments, "width", nw)
        mean = sums[0] / dim
        inv_std = lax.rsqrt(sums[1] / dim - mean * mean + 1e-06)
        stats = jnp.stack([mean, inv_std], 1)

        unit = count // sum(SPLIT)
        chunks, start = [], 0
        for s in SPLIT:
            chunks.append((start, s * unit))
            start += s * unit
        core_arr = core.astype(jnp.int32)[None]
        near, flip = [], []
        for at, n in chunks:
            tiles = n // TILE
            near += [at // TILE + t for t in range(tiles)]
            flip += [at // TILE + (t + tiles // 2) % tiles for t in range(tiles)]
        order = jnp.where(core == 0, jnp.array(near, jnp.int32), jnp.array(flip, jnp.int32))

        def plain(rows, cols):
            return pl.BlockSpec((rows, cols), lambda j, *_: (0, 0))

        def rows_spec(cols):
            return pl.BlockSpec((TILE, cols), lambda j, *_: (j, 0))

        pieces = [(at + side * (n // 2), n // 2) for at, n in chunks for side in range(2)]
        steps = pl.cdiv(fh, BLOCK_N)

        anywhere = pl.BlockSpec(memory_space=pl.ANY)

        def project(kernel, ins, specs, w, extra):
            return call(
                functools.partial(kernel, pieces), (steps,), 1,
                [anywhere] + specs + [pl.BlockSpec((BLOCK_N, dw), lambda j, *_: (j, 0))],
                [plain(*e.shape) for e in extra]
                + [pl.BlockSpec((size, BLOCK_N), lambda j, *_: (0, j)) for _, size in pieces],
                extra + [shape((size, fh)) for _, size in pieces],
                (count * fh * dw * 2, fh * dw * 2 + count * (fh + 3 * dw) * 2),
            )(order, *ins, w)

        pairs = [None] * (2 * len(chunks))

        def exchange(i, k, parts, dep):
            own, oth = parts[2 * i:2 * i + 2]
            own, got = tie((own, swap(oth, "width", 1, nw)), dep)
            value = bf16(f32(own) + f32(got))
            dep = value
            mask = 2
            while 2 * mask < nw:
                value = bf16(f32(value) + f32(swap(value, "width", mask, nw)))
                mask *= 2
            pairs[2 * i + k] = (value, swap(value, "width", mask, nw))
            return dep

        d_all, cot_all, hot_all, *d_parts = project(
            project_d_kernel, [moments, cotangent, seg, gate3],
            [plain(count, dw), plain(count, 1), plain(3 * reqs, dw)], w_down,
            [shape((count, dw)), shape((count, dw)), shape((count, 128))],
        )
        last_chunk = len(chunks) - 1
        dep = exchange(0, 0, d_parts, d_parts[0])
        dep = exchange(last_chunk, 0, d_parts, dep)
        w_up_t = w_up.T
        n_all, *u_parts = project(
            project_u_kernel, [dep, tokens, seg, stats, shift3, scale3],
            [plain(count, dw), plain(count, 1), plain(count, 2)] + [plain(3 * reqs, dw)] * 2, w_up_t,
            [shape((count, dw))],
        )
        dep = exchange(0, 1, u_parts, u_parts[0])
        for i in range(1, len(chunks)):
            if i < last_chunk:
                dep = exchange(i, 0, d_parts, dep)
            dep = exchange(i, 1, u_parts, dep)

        masks = []
        while 2 ** len(masks) < nh:
            masks.append(2 ** len(masks))
        bits = [(me // mask) % 2 for mask in masks]
        spot = 0
        for bit in bits:
            spot = spot * 2 + bit
        xbit = bits[0]
        flag = (xbit == core).astype(jnp.int32)[None]
        spot_arr = spot.astype(jnp.int32)[None]
        bias_row = bias_up[None]
        state = {"bias": 0.0, "table": 0.0, "buffers": [], "out": jnp.zeros((count, dw), jnp.bfloat16)}
        boths, gots, feats, grads = {}, {}, {}, {}

        def mid(i, dep):
            half = chunks[i][1] // 2
            both, total = call(
                mid_kernel, (half // TILE,), 0,
                [anywhere] + [rows_spec(fh)] * 4 + [plain(1, fh)],
                [pl.BlockSpec((2, TILE, fh), lambda j: (0, j, 0)), plain(1, fh)],
                [shape((2, half, fh)), shape((1, fh), jnp.float32)], (half * fh * 30, half * fh * 12),
            )(dep, *pairs[2 * i], *pairs[2 * i + 1], bias_row)
            state["bias"] = state["bias"] + total[0]
            boths[i] = (both, swap(both, "width", 1, nw))
            return total

        def part(i, dep):
            at, n = chunks[i]
            half = n // 2
            buffers = state["buffers"]
            cols = BLOCK_D if dw % BLOCK_D == 0 else dw
            whole = pl.BlockSpec((2, half, fh), lambda j, *_: (0, 0, 0))
            here = pl.BlockSpec((n, fh), lambda j, *_: (at // n, 0))
            send, keep, *buffers = call(
                functools.partial(part_kernel, not buffers), (dw // cols,), 1,
                [anywhere, whole, whole, pl.BlockSpec((fh, cols), lambda j, *_: (0, j))] + [anywhere] * len(buffers),
                [pl.BlockSpec((half, cols), lambda j, *_: (0, j))] * 2 + [here, here],
                [shape((half, dw)), shape((half, dw)), shape((count, fh)), shape((count, fh))],
                (n * fh * dw * 2, n * fh * 8 + fh * dw * 2 + n * dw * 2),
                {5: 2, 6: 3} if buffers else None,
            )(flag, dep, *boths[i], w_up_t, *buffers)
            state["buffers"] = buffers
            gots[i] = (keep, swap(send, "hidden", 1, nh))
            return keep

        def halve(i, dep, which):
            for k in which:
                keep, got = tie(gots[i], dep)
                value = (f32(keep) + f32(got)).reshape(2, -1, dw)
                send = bf16(lax.dynamic_index_in_dim(value, 1 - bits[k], 0, keepdims=False))
                dep = send
                got = swap(send, "hidden", masks[k], nh)
                gots[i] = (lax.dynamic_index_in_dim(value, bits[k], 0, keepdims=False), got)
            return dep

        def double(i, dep, which):
            for k in which:
                grad, got = tie(grads[i], dep)
                grad = jnp.where(bits[k] == 0, jnp.stack([grad, got]), jnp.stack([got, grad])).reshape(-1, dw)
                dep = grad
                grads[i] = (grad, swap(grad, "hidden", masks[k - 1], nh))
            return dep

        def places(i):
            at, n = chunks[i]
            rows = n // nh
            if rows % 16 == 0 and at % rows == 0:
                return rows, lambda v: v, lambda cols: pl.BlockSpec((rows, cols), lambda j, q: (at // rows + q[0], 0))
            return rows, lambda v: lax.dynamic_slice_in_dim(v, at + spot * rows, rows, 0), lambda cols: plain(rows, cols)

        def norm_a(i, dep):
            rows, mine, own_spec = places(i)
            sums_part, table_new = call(
                norm_a_kernel, (1,), 1,
                [anywhere, plain(rows, dw), plain(rows, dw), own_spec(dw), own_spec(2), own_spec(1), plain(3 * reqs, dw)],
                [plain(rows, 128), pl.BlockSpec((2, reqs, dw), lambda j, *_: (0, 0, 0))],
                [shape((rows, 128), jnp.float32), shape((2, reqs, dw), jnp.float32)],
                (rows * dw * 200, rows * dw * 16),
            )(spot_arr, dep, *gots[i], mine(tokens), mine(stats), mine(seg), scale3)
            state["table"] = state["table"] + table_new
            feats[i] = sum_all(sums_part, "width", nw)
            return sums_part

        def norm_b(i, dep):
            rows, mine, own_spec = places(i)
            grad = call(
                functools.partial(norm_b_kernel, dim), (1,), 1,
                [anywhere, plain(rows, dw), plain(rows, dw), own_spec(dw), own_spec(dw), own_spec(2), own_spec(1), plain(3 * reqs, dw), plain(rows, 128)],
                plain(rows, dw), shape((rows, dw)), (rows * dw * 200, rows * dw * 12),
            )(spot_arr, dep, *gots[i], mine(tokens), mine(cotangent), mine(stats), mine(seg), scale3, feats[i])
            grads[i] = (grad, swap(grad, "hidden", masks[-1], nh))
            return grad

        def finish(i, dep):
            at, n = chunks[i]
            grad, other = tie(grads[i], dep)
            out = lax.dynamic_update_slice(state["out"], grad, (at + xbit * (n // 2), 0))
            state["out"] = lax.dynamic_update_slice(out, other, (at + (1 - xbit) * (n // 2), 0))
            return grad

        def down(i, dep):
            act_all, = tie((state["buffers"][0],), dep)
            state["down"] = mm(act_all, d_all, ((0,), (0,)))
            return state["down"]

        def up(i, dep):
            grad_all, = tie((state["buffers"][1],), dep)
            state["up"] = mm(grad_all, n_all, ((0,), (0,)))
            return state["up"]

        def gate(i, dep):
            act_all, = tie((state["buffers"][0],), dep)
            y_cot = bf16(f32(cot_all) * mm(act_all, w_down, ((1,), (0,))))
            state["gate"] = mm(hot_all, y_cot, ((0,), (0,)))[:reqs]
            return state["gate"]

        count_masks = len(masks)
        stages = {
            "mid": mid, "part": part, "na": norm_a, "nb": norm_b, "fin": finish, "down": down, "up": up, "gate": gate,
            "ra": lambda i, dep: halve(i, dep, range(1, 2)),
            "rb": lambda i, dep: halve(i, dep, range(2, count_masks)),
            "ga": lambda i, dep: double(i, dep, range(count_masks - 1, 1, -1)),
            "gb": lambda i, dep: double(i, dep, range(1, 0, -1)),
        }
        for stage, i in PLAN:
            dep = stages[stage](i, dep)

        table = sum_pairs(jnp.concatenate([state["table"], state["gate"][None]], 0), "hidden", 1, nh)
        grad_table = jnp.einsum("rk,crd->kcd", step_of, table, precision=highest)
        grad_bias = state["bias"] + swap(state["bias"], "width", 1, nw)
        return state["out"], state["up"].T, state["down"], grad_bias, grad_table

    return body


def solution(mesh):
    body = make_body(mesh.shape["width"], mesh.shape["hidden"])

    return jax.shard_map(
        body,
        mesh=mesh,
        in_specs=(
            P(None, "width"),
            P(None, "width"),
            P("width", "hidden"),
            P("hidden"),
            P("hidden", "width"),
            P(None, None, "width"),
            P(),
            P(),
        ),
        out_specs=(
            P(None, "width"),
            P("width", "hidden"),
            P("hidden", "width"),
            P("hidden"),
            P(None, None, "width"),
        ),
        check_vma=False,
    )
```

```python
import functools

import jax
import jax.numpy as jnp
from jax import lax
from jax.experimental import pallas as pl
from jax.experimental.pallas import tpu as pltpu
from jax.sharding import PartitionSpec as P


SPLIT = (3, 4, 2)
TILE = 64
BLOCK_N = 896
GROUPS = ((0,), (1, 2))
BLOCK_D = 640
EXTRA = 128
PLAN = tuple(
    (word.rstrip("0123456789"), int(word[-1]))
    for line in (
        "mid0 part0 mid1 ra0",
        "part1 rb0 mid2 part2",
        "nb0 ra1 gate0 ra2",
        "ga0 rb1 down0 rb2",
        "gb0 nb1 nb2 t0",
        "ga1 ga2 t1 gb2",
        "gb1 t2 up0 fin0",
        "fin1 fin2",
    )
    for word in line.split()
)


def f32(value):
    return value.astype(jnp.float32)


def bf16(value):
    return value.astype(jnp.bfloat16)


def swap(value, axis, mask, size):
    return lax.ppermute(value, axis, [(i, i ^ mask) for i in range(size)])


def sum_all(value, axis, size):
    terms = [value] + [swap(value, axis, mask, size) for mask in range(1, size)]
    while len(terms) > 1:
        terms = [terms[i] + terms[i + 1] for i in range(0, len(terms), 2)]
    return terms[0]


def round_off(value):
    return lax.reduce_precision(value, 8, 7)


def three_parts(value):
    first = round_off(value)
    second = round_off(value - first)
    third = value - first - second
    return bf16(jnp.concatenate([first, second, third], 0))


def mm(a, b, dims):
    return lax.dot_general(a, b, (dims, ((), ())), preferred_element_type=jnp.float32)


def tie(values, other):
    values = list(values)
    *values, _ = lax.optimization_barrier((*values, other))
    return values


def look(seg, table):
    wide = table.shape[0]
    reqs = wide // 3
    lanes = lax.broadcasted_iota(jnp.int32, (seg.shape[0], wide), 1)
    hot = (lanes == seg) | (lanes == seg + reqs) | (lanes == seg + 2 * reqs)
    return mm(jnp.where(hot, 1.0, 0.0).astype(jnp.bfloat16), table, ((1,), (0,)))


def call(kernel, grid, prefetch, in_specs, out_specs, out_shape, cost, aliases=None):
    return pl.pallas_call(
        kernel,
        out_shape=out_shape,
        grid_spec=pltpu.PrefetchScalarGridSpec(
            num_scalar_prefetch=prefetch, grid=grid, in_specs=in_specs, out_specs=out_specs
        ),
        input_output_aliases=aliases or {},
        cost_estimate=pl.CostEstimate(flops=cost[0], bytes_accessed=cost[1], transcendentals=0),
    )


def shape(dims, dtype=jnp.bfloat16):
    return jax.ShapeDtypeStruct(dims, dtype)


def project_pieces(pieces, lhs, w, outs):
    total = bf16(mm(lhs[...], w[...], ((1,), (1,))))
    for (start, size), out in zip(pieces, outs):
        out[...] = total[start:start + size]


def project_d_kernel(pieces, first, order, dep, cot, seg, gate, w, *refs):
    lhs, cot_out, hot_out, *outs = refs[0 if first else 3:]

    @pl.when(pl.program_id(0) == 0)
    def _():
        def step(t, carry):
            src = pl.ds(pl.multiple_of(order[t] * TILE, TILE), TILE)
            dst = pl.ds(pl.multiple_of(t * TILE, TILE), TILE)
            ids = seg[src, :]
            value = cot[src, :]
            lhs[dst, :] = bf16(f32(value) * look(ids, gate[...]))
            cot_out[dst, :] = value
            lanes = lax.broadcasted_iota(jnp.int32, (TILE, hot_out.shape[1]), 1)
            hot_out[dst, :] = jnp.where(lanes == ids, 1.0, 0.0).astype(jnp.bfloat16)
            return carry

        lax.fori_loop(0, lhs.shape[0] // TILE, step, 0)

    project_pieces(pieces, lhs, w, outs)


def project_u_kernel(pieces, first, order, dep, tok, seg, st, shift, scale, w, *refs):
    lhs, *outs = refs[0 if first else 1:]

    @pl.when(pl.program_id(0) == 0)
    def _():
        def step(t, carry):
            src = pl.ds(pl.multiple_of(order[t] * TILE, TILE), TILE)
            dst = pl.ds(pl.multiple_of(t * TILE, TILE), TILE)
            ids = seg[src, :]
            x_hat = (f32(tok[src, :]) - st[src, 0:1]) * st[src, 1:2]
            lhs[dst, :] = bf16(x_hat * (1.0 + look(ids, scale[...])) + look(ids, shift[...]))
            return carry

        lax.fori_loop(0, lhs.shape[0] // TILE, step, 0)

    project_pieces(pieces, lhs, w, outs)


def mid_kernel(core, dep, ds, dr, us, ur, bias, seg, mixes, out, total):
    fh = bias.shape[1]
    linear = f32(us[:, :fh]) + f32(ur[:, :fh])
    value = linear + bias[...]
    root = 0.7978845608028654
    square = value * value
    bent = jnp.tanh(value * (root + (0.044715 * root) * square))
    half = 0.5 + 0.5 * bent
    slope = half + value * (0.5 - 0.5 * (bent * bent)) * (root + (0.134145 * root) * square)
    d_pre = (f32(ds[:, :fh]) + f32(dr[:, :fh])) * slope
    rounded = bf16(d_pre)
    out[0, :, :fh] = bf16(value * half)
    out[1, :, :fh] = rounded
    kinds = mm(rounded, mixes[...], ((1,), (1,)))
    reqs = kinds.shape[1] // 2
    lanes = lax.broadcasted_iota(jnp.int32, kinds.shape, 1)
    one = jnp.sum(jnp.where(lanes == seg[...], kinds, 0.0), 1, keepdims=True)
    two = jnp.sum(d_pre * linear, 1, keepdims=True)
    two = two - jnp.sum(jnp.where(lanes == seg[...] + reqs, kinds, 0.0), 1, keepdims=True)
    spare = out.shape[2] - fh
    place = lax.broadcasted_iota(jnp.int32, (one.shape[0], spare), 1)
    both = jnp.where((place & 1) == 0, one, two)
    high = bf16(both)
    out[1, :, fh:] = bf16(jnp.where(place < 2, f32(high), jnp.where(place < 4, both - f32(high), 0.0)))
    out[0, :, fh:] = jnp.zeros((one.shape[0], spare), jnp.bfloat16)

    @pl.when(pl.program_id(0) == 0)
    def _():
        total[...] = jnp.zeros_like(total)

    total[...] += jnp.sum(d_pre, 0, keepdims=True)


def part_kernel(first, flags, dep, own, oth, w, *refs):
    send, keep, act_all, grad_all = refs[0 if first else 2:]
    half = own.shape[1]
    fh = w.shape[0]
    step = pl.program_id(0)

    @pl.when(step == 0)
    def _():
        for side, ref in enumerate((own, oth)):
            act_all[side * half:(side + 1) * half, :] = ref[0, :, :fh]
            grad_all[side * half:(side + 1) * half, :] = ref[1, :, :fh]

    def put(lower, upper, cols):
        @pl.when(flags[0] == 1)
        def _():
            send[:, :cols] = upper
            keep[:, :cols] = lower

        @pl.when(flags[0] == 0)
        def _():
            send[:, :cols] = lower
            keep[:, :cols] = upper

    @pl.when(step < pl.num_programs(0) - 1)
    def _():
        total = bf16(mm(grad_all[...], w[...], ((1,), (0,))))
        put(total[:half], total[half:], w.shape[1])

    @pl.when(step == pl.num_programs(0) - 1)
    def _():
        spare = own.shape[2] - fh
        wide = jnp.zeros((half, EXTRA - spare), jnp.bfloat16)
        put(*[jnp.concatenate([ref[1, :, fh:], wide], 1) for ref in (own, oth)], EXTRA)


def norm_kernel(dim, q, dep, keep, got, tok, cot, st, seg, scale, out, table):
    dw = tok.shape[1]
    d = keep[:, :dw] + f32(got[:, :dw])
    sums = (keep[:, dw:] + f32(got[:, dw:])) * (1.0 / dim)
    one = sums[:, 0:1] + sums[:, 2:3]
    two = sums[:, 1:2] + sums[:, 3:4]
    inv = st[:, 1:2]
    x_hat = (f32(tok[...]) - st[:, 0:1]) * inv
    d_hat = d * (1.0 + look(seg[...], scale[...]))
    out[...] = bf16(f32(cot[...]) + inv * (d_hat - one - x_hat * two))
    reqs = table.shape[1]
    ids = lax.broadcasted_iota(jnp.int32, (d.shape[0], reqs), 1)
    hot = jnp.where(ids == seg[...], 1.0, 0.0).astype(jnp.bfloat16)
    for c, value in enumerate((d, d * x_hat)):
        top = bf16(value)
        low = bf16(value - f32(top))
        table[c] = mm(hot, top, ((0,), (0,))) + mm(hot, low, ((0,), (0,)))


def make_body(nw, nh):
    def body(tokens, cotangent, w_up, bias_up, w_down, mod_table, seg_ids, step_ids):
        count, dw = tokens.shape
        fh = w_up.shape[1]
        dim = dw * nw
        reqs, rows_of = step_ids.shape[0], mod_table.shape[0]
        highest = lax.Precision.HIGHEST
        core = lax.axis_index("width") % 2
        me = lax.axis_index("hidden")
        step_of = f32(step_ids[:, None] == jnp.arange(rows_of)[None, :])
        req_mod = jnp.einsum("rk,kcd->crd", step_of, mod_table, precision=highest)
        shift3, scale3, gate3 = [three_parts(req_mod[c]) for c in range(3)]
        seg = seg_ids[:, None]

        mixes = bf16(jnp.concatenate([1.0 + req_mod[1], req_mod[0]], 0))
        mixes = bf16(mm(mixes, w_up, ((1,), (0,))))
        unit = count // sum(SPLIT)
        chunks, start = [], 0
        for s in SPLIT:
            chunks.append((start, s * unit))
            start += s * unit
        core_arr = core.astype(jnp.int32)[None]
        groups = GROUPS
        stores, spot_now = {}, 0
        for group in reversed(groups):
            for i in group:
                stores[i] = spot_now
                spot_now += chunks[i][1]
        orders = []
        for group in groups:
            near, flip = [], []
            for i in group:
                at, n = chunks[i]
                tiles = n // TILE
                near += [at // TILE + t for t in range(tiles)]
                flip += [at // TILE + (t + tiles // 2) % tiles for t in range(tiles)]
            orders.append(jnp.where(core == 0, jnp.array(near, jnp.int32), jnp.array(flip, jnp.int32)))

        def plain(rows, cols):
            return pl.BlockSpec((rows, cols), lambda j, *_: (0, 0))

        def rows_spec(cols):
            return pl.BlockSpec((TILE, cols), lambda j, *_: (j, 0))

        fhx = pl.cdiv(fh + 4, 128) * 128
        block_n = min(BLOCK_N, fhx)
        steps = pl.cdiv(fhx, block_n)
        anywhere = pl.BlockSpec(memory_space=pl.ANY)

        def project(kernel, g, ins, specs, w, extra, parts, buffers):
            base = stores[groups[g][0]]
            rows = sum(chunks[i][1] for i in groups[g])
            pieces = [(stores[i] - base + side * (chunks[i][1] // 2), chunks[i][1] // 2)
                      for i in groups[g] for side in range(2)]
            kept = len(extra)
            *outs, = call(
                functools.partial(kernel, pieces, not buffers), (steps,), 1,
                [anywhere] + specs + [pl.BlockSpec((block_n, dw), lambda j, *_: (j, 0))] + [anywhere] * len(buffers),
                [pl.BlockSpec((rows, cols), lambda j, *_: (base // rows, 0)) for cols in extra]
                + [pl.BlockSpec((size, block_n), lambda j, *_: (0, j)) for _, size in pieces],
                [shape((count, cols)) for cols in extra] + [shape((size, fhx)) for _, size in pieces],
                (rows * fh * dw * 2, fh * dw * 2 + rows * (fh + 3 * dw) * 2),
                {len(ins) + 2 + k: k for k in range(len(buffers))},
            )(orders[g], *ins, w, *buffers)
            for k, i in enumerate(groups[g]):
                parts[i] = outs[kept + 2 * k:kept + 2 * k + 2]
            return outs[:kept]

        d_parts, u_parts = {}, {}

        def project_d(g, dep, buffers):
            return project(
                project_d_kernel, g, [dep, cotangent, seg, gate3],
                [plain(count, dw), plain(count, 1), plain(3 * reqs, dw)], w_down, [dw, dw, 128], d_parts, buffers,
            )

        def project_u(g, dep, buffers):
            return project(
                project_u_kernel, g, [dep, tokens, seg, stats, shift3, scale3],
                [plain(count, dw), plain(count, 1), plain(count, 2)] + [plain(3 * reqs, dw)] * 2, w_up_t, [dw],
                u_parts, buffers,
            )

        w_up_t = w_up.T
        pairs = [None] * (2 * len(chunks))

        def exchange(i, k, parts, dep):
            own, oth = parts[i]
            own, got = tie((own, swap(oth, "width", 1, nw)), dep)
            value = bf16(f32(own) + f32(got))
            dep = value
            mask = 2
            while 2 * mask < nw:
                value = bf16(f32(value) + f32(swap(value, "width", mask, nw)))
                mask *= 2
            pairs[2 * i + k] = (value, swap(value, "width", mask, nw))
            return dep

        d_bufs = project_d(0, core_arr, [])
        late, = tie((tokens,), d_bufs[0])
        x_full = f32(late)
        moments = jnp.stack([jnp.sum(x_full, 1), jnp.sum(x_full * x_full, 1)])
        sums = sum_all(moments, "width", nw)
        mean = sums[0] / dim
        inv_std = lax.rsqrt(sums[1] / dim - mean * mean + 1e-06)
        stats = jnp.stack([mean, inv_std], 1)
        dep = exchange(0, 0, d_parts, d_bufs[0])
        n_bufs = project_u(0, dep, [])
        mixes, = tie((mixes,), n_bufs[0])
        mask = 1
        while mask < nw:
            mixes = bf16(f32(mixes) + f32(swap(mixes, "width", mask, nw)))
            mask *= 2
        dep = exchange(0, 1, u_parts, n_bufs[0])
        d_all, cot_all, hot_all = project_d(1, dep, d_bufs)
        dep = exchange(1, 0, d_parts, d_all)
        n_all, = project_u(1, dep, n_bufs)
        dep = n_all
        for i in range(1, len(chunks)):
            if i > 1:
                dep = exchange(i, 0, d_parts, dep)
            dep = exchange(i, 1, u_parts, dep)

        masks = []
        while 2 ** len(masks) < nh:
            masks.append(2 ** len(masks))
        bits = [(me // mask) % 2 for mask in masks]
        spot = 0
        for bit in bits:
            spot = spot * 2 + bit
        xbit = bits[0]
        flag = (xbit == core).astype(jnp.int32)[None]
        spot_arr = spot.astype(jnp.int32)[None]
        bias_row = bias_up[None]
        dwx = dw + EXTRA
        state = {"bias": 0.0, "table": 0.0, "buffers": [], "out": jnp.zeros((count, dw), jnp.bfloat16)}
        boths, gots, grads = {}, {}, {}

        def mid(i, dep):
            half = chunks[i][1] // 2
            at = chunks[i][0]
            both, total = call(
                mid_kernel, (half // TILE,), 1,
                [anywhere] + [rows_spec(fhx)] * 4 + [plain(1, fh)]
                + [pl.BlockSpec((TILE, 1), lambda j, c: ((at + c[0] * half) // TILE + j, 0)), plain(2 * reqs, fh)],
                [pl.BlockSpec((2, TILE, fhx), lambda j, *_: (0, j, 0)), plain(1, fh)],
                [shape((2, half, fhx)), shape((1, fh), jnp.float32)], (half * fh * 30, half * fh * 12),
            )(core_arr, dep, *pairs[2 * i], *pairs[2 * i + 1], bias_row, seg, mixes)
            state["bias"] = state["bias"] + total[0]
            boths[i] = (both, swap(both, "width", 1, nw))
            return total

        def part(i, dep):
            _, n = chunks[i]
            half = n // 2
            buffers = state["buffers"]
            cols = BLOCK_D if dw % BLOCK_D == 0 else dw
            last = dw // cols - 1
            whole = pl.BlockSpec((2, half, fhx), lambda j, *_: (0, 0, 0))
            store = stores[i]
            here = pl.BlockSpec((n, fh), lambda j, *_: (store // n, 0))
            send, keep, *buffers = call(
                functools.partial(part_kernel, not buffers), (last + 2,), 1,
                [anywhere, whole, whole, pl.BlockSpec((fh, cols), lambda j, *_: (0, jnp.minimum(j, last)))]
                + [anywhere] * len(buffers),
                [pl.BlockSpec((half, cols), lambda j, *_: (0, j))] * 2 + [here, here],
                [shape((half, dwx)), shape((half, dwx)), shape((count, fh)), shape((count, fh))],
                (n * fh * dw * 2, n * fh * 8 + fh * dw * 2 + n * dw * 2),
                {5: 2, 6: 3} if buffers else None,
            )(flag, dep, *boths[i], w_up_t, *buffers)
            state["buffers"] = buffers
            gots[i] = (keep, swap(send, "hidden", 1, nh))
            return keep

        def halve(i, dep, which):
            for k in which:
                keep, got = tie(gots[i], dep)
                value = (f32(keep) + f32(got)).reshape(2, -1, dwx)
                send = bf16(lax.dynamic_index_in_dim(value, 1 - bits[k], 0, keepdims=False))
                dep = send
                got = swap(send, "hidden", masks[k], nh)
                gots[i] = (lax.dynamic_index_in_dim(value, bits[k], 0, keepdims=False), got)
            return dep

        def double(i, dep, which):
            for k in which:
                grad, got = tie(grads[i], dep)
                grad = jnp.where(bits[k] == 0, jnp.stack([grad, got]), jnp.stack([got, grad])).reshape(-1, dw)
                dep = grad
                grads[i] = (grad, swap(grad, "hidden", masks[k - 1], nh))
            return dep

        def places(i):
            at, n = chunks[i]
            rows = n // nh
            if rows % 16 == 0 and at % rows == 0:
                return rows, lambda v: v, lambda cols: pl.BlockSpec((rows, cols), lambda j, q: (at // rows + q[0], 0))
            return rows, lambda v: lax.dynamic_slice_in_dim(v, at + spot * rows, rows, 0), lambda cols: plain(rows, cols)

        def norm(i, dep):
            rows, mine, own_spec = places(i)
            grad, table_new = call(
                functools.partial(norm_kernel, dim), (1,), 1,
                [anywhere, plain(rows, dwx), plain(rows, dwx), own_spec(dw), own_spec(dw), own_spec(2), own_spec(1),
                 plain(3 * reqs, dw)],
                [plain(rows, dw), pl.BlockSpec((2, reqs, dw), lambda j, *_: (0, 0, 0))],
                [shape((rows, dw)), shape((2, reqs, dw), jnp.float32)], (rows * dw * 300, rows * dw * 16),
            )(spot_arr, dep, *gots[i], mine(tokens), mine(cotangent), mine(stats), mine(seg), scale3)
            state["table"] = state["table"] + table_new
            grads[i] = (grad, swap(grad, "hidden", masks[-1], nh))
            return grad

        def finish(i, dep):
            at, n = chunks[i]
            grad, other = tie(grads[i], dep)
            out = lax.dynamic_update_slice(state["out"], grad, (at + xbit * (n // 2), 0))
            state["out"] = lax.dynamic_update_slice(out, other, (at + (1 - xbit) * (n // 2), 0))
            return grad

        def down(i, dep):
            act_all, = tie((state["buffers"][0],), dep)
            state["down"] = mm(act_all, d_all, ((0,), (0,)))
            return state["down"]

        def up(i, dep):
            grad_all, = tie((state["buffers"][1],), dep)
            state["up"] = mm(grad_all, n_all, ((0,), (0,)))
            return state["up"]

        def gate(i, dep):
            act_all, = tie((state["buffers"][0],), dep)
            y_cot = bf16(f32(cot_all) * mm(act_all, w_down, ((1,), (0,))))
            state["gate"] = mm(hot_all, y_cot, ((0,), (0,)))[:reqs]
            return state["gate"]

        def gather_table(i, dep):
            if i == 0:
                state["sum"] = jnp.concatenate([state["table"], state["gate"][None]], 0)
                which = range(1)
            else:
                which = range(i, i + 1) if i < 2 else range(2, len(masks))
            for k in which:
                mine = bf16(state["sum"])
                mine, = tie((mine,), dep)
                other = swap(mine, "hidden", masks[k], nh)
                state["sum"] = f32(mine) + f32(other)
                dep = mine
            return dep

        count_masks = len(masks)
        stages = {
            "mid": mid, "part": part, "nb": norm, "fin": finish, "down": down, "up": up, "gate": gate, "t": gather_table,
            "ra": lambda i, dep: halve(i, dep, range(1, 2)),
            "rb": lambda i, dep: halve(i, dep, range(2, count_masks)),
            "ga": lambda i, dep: double(i, dep, range(count_masks - 1, 1, -1)),
            "gb": lambda i, dep: double(i, dep, range(1, 0, -1)),
        }
        for stage, i in PLAN:
            dep = stages[stage](i, dep)

        grad_table = jnp.einsum("rk,crd->kcd", step_of, state["sum"], precision=highest)
        grad_bias = state["bias"] + swap(state["bias"], "width", 1, nw)
        return state["out"], state["up"].T, state["down"], grad_bias, grad_table

    return body


def solution(mesh):
    body = make_body(mesh.shape["width"], mesh.shape["hidden"])

    return jax.shard_map(
        body,
        mesh=mesh,
        in_specs=(
            P(None, "width"),
            P(None, "width"),
            P("width", "hidden"),
            P("hidden"),
            P("hidden", "width"),
            P(None, None, "width"),
            P(),
            P(),
        ),
        out_specs=(
            P(None, "width"),
            P("width", "hidden"),
            P("hidden", "width"),
            P("hidden"),
            P(None, None, "width"),
        ),
        check_vma=False,
    )
```
